32 devices in a mesh: bucket: 16 (over z, y, core), edge: 2 (over x).
Axes of the slice: x: 2, y: 2, z: 4, core: 2. Of those that a mesh axis runs over, the one named last changes fastest.
Arguments:
- left_slab: bfloat16 [6144, 256], P(('bucket', 'edge')), may hold values from -1.5 to 1.5
- right_slab: bfloat16 [6144, 256], P(('bucket', 'edge')), may hold values from -1.5 to 1.5
- relation: float32 [1024, 256], replicated, may hold values from 0.5 to 1.5
- src_ids: int32 [2, 16, 4096], P(None, 'bucket', 'edge'), may hold values from 0 to 383
- dst_ids: int32 [2, 16, 4096], P(None, 'bucket', 'edge'), may hold values from 0 to 383
- rel_ids: int32 [2, 16, 4096], P(None, 'bucket', 'edge'), may hold values from 0 to 1023
- neg_ids: int32 [2, 16, 16, 512], P(None, 'bucket', 'edge'), may hold values from 0 to 383
- edge_counts: int32 [2, 16], P(None, 'bucket'), may hold values from 1 to 4096, as said below
Outputs:
- left_out: bfloat16 [6144, 256], P(('bucket', 'edge'))
- right_out: bfloat16 [6144, 256], P(('bucket', 'edge'))
- relation_out: float32 [1024, 256], replicated
The draws below stay inside these ranges and needn't reach their ends.
Inputs may be any that keep to these rules, and one draw needn't show every extreme that they name: `edge_counts`: live edges are the first slots of a bucket; in every round some bucket has all 4096 slots live.
All inputs are finite; a program needn't handle non-finite values.
Results may differ from the reference program's by a relative error of at most 0.0046.
Values may be sent and summed in bfloat16 or wider, within the bound.
A program may use at most 64 MiB of HBM per device.

```python
import jax
import jax.numpy as jnp
from jax import lax

W = 256
RELS = 1024
SPAN = 256
NEG = 512
ROUNDS = 2
SPANS_DEV = 8
GROUPS = 16
SLAB = 384
CAP = 4096
N_EDGE = 2


def draw_edge_counts(key, part):
    key_base = jax.random.fold_in(key, 11)
    key_full = jax.random.fold_in(key, 12)
    base = jax.random.randint(key_base, (ROUNDS, GROUPS), CAP // 8, CAP // 2 + 1)
    full = jax.random.randint(key_full, (ROUNDS,), 0, GROUPS)
    chosen = jnp.arange(GROUPS)[None, :] == full[:, None]
    return jnp.where(chosen, CAP, base).astype(jnp.int32)


def touch_ends(array, key, low, top_value):
    shape = array.shape
    index_at = [jax.random.randint(jax.random.fold_in(key, axis), (), 0, shape[axis]) for axis in range(len(shape))]
    array = array.at[tuple(index_at)].set(low)
    longest = shape.index(max(shape))
    index_at[longest] = (index_at[longest] + 1) % shape[longest]
    return array.at[tuple(index_at)].set(top_value)


def block_scale(rng, shape, cuts, smallest, high):
    loudness, own = 1.0, jax.random.fold_in(rng, 6)
    for axis_at, parts in cuts:
        draws = jnp.exp(jax.random.uniform(jax.random.fold_in(own, axis_at), (parts,), jnp.float32, smallest / len(cuts), high / len(cuts)))
        loudness = loudness * jnp.repeat(draws, shape[axis_at] // parts).reshape([-1 if axis == axis_at else 1 for axis in range(len(shape))])
    return loudness


def scatter_about(key, extent, width, most, pieces=(), kind=jnp.bfloat16):
    result = jax.random.normal(key, extent, jnp.float32) * width
    if len(pieces) > 0:
        result = block_scale(key, extent, pieces, -0.22, 0.18) * result
    return jnp.clip(result, min=-most, max=most).astype(kind)


def setup_inputs(seed: int = 0) -> dict:
    arg_keys = jax.random.split(jax.random.key(seed), 9)
    left_slab = scatter_about(arg_keys[0], (GROUPS * SLAB, W), 0.25, 1.5, ((0, 32),))
    right_slab = scatter_about(arg_keys[1], (GROUPS * SLAB, W), 0.25, 1.5, ((0, 32),))
    relation = jnp.clip(jax.random.uniform(arg_keys[2], (RELS, W), jnp.float32, 0.5, 1.5), 0.5, 1.5)
    src_ids = touch_ends(jax.random.randint(arg_keys[3], (ROUNDS, GROUPS, CAP), 0, SLAB), jax.random.fold_in(arg_keys[3], 1), 0, SLAB - 1).astype(jnp.int32)
    dst_ids = touch_ends(jax.random.randint(arg_keys[4], (ROUNDS, GROUPS, CAP), 0, SLAB), jax.random.fold_in(arg_keys[4], 1), 0, SLAB - 1).astype(jnp.int32)
    rel_ids = touch_ends(jax.random.randint(arg_keys[5], (ROUNDS, GROUPS, CAP), 0, RELS), jax.random.fold_in(arg_keys[5], 1), 0, RELS - 1).astype(jnp.int32)
    neg_ids = touch_ends(jax.random.randint(arg_keys[6], (ROUNDS, GROUPS, SPANS_DEV * N_EDGE, NEG), 0, SLAB), jax.random.fold_in(arg_keys[6], 1), 0, SLAB - 1).astype(jnp.int32)
    edge_counts = draw_edge_counts(jax.random.fold_in(arg_keys[8], 71), 0)
    return dict(left_slab=left_slab, right_slab=right_slab, relation=relation, src_ids=src_ids, dst_ids=dst_ids, rel_ids=rel_ids, neg_ids=neg_ids, edge_counts=edge_counts)


learn_rate = 0.05
relation_rate = 0.05


def span_grads(left, right, theta, src_c, dst_c, rel_c, neg_c, mask):
    s_rows = left[src_c]
    d_rows = right[dst_c]
    negatives = right[neg_c]
    t_rows = theta[rel_c]
    s_wide = s_rows.astype(jnp.float32)
    q_rows = (s_wide * t_rows).astype(jnp.bfloat16)
    q_wide = q_rows.astype(jnp.float32)
    d_wide = d_rows.astype(jnp.float32)
    pos = jnp.sum(q_wide * d_wide, axis=-1)
    scores = jnp.dot(q_rows, negatives.T, preferred_element_type=jnp.float32)
    g_pos = -jax.nn.sigmoid(-pos) * mask
    g_neg = (jax.nn.sigmoid(scores) * mask[:, None]).astype(jnp.bfloat16)
    g_q = g_pos[:, None] * d_wide + jnp.dot(g_neg, negatives, preferred_element_type=jnp.float32)
    g_d = g_pos[:, None] * q_wide
    g_negrows = jnp.dot(g_neg.T, q_rows, preferred_element_type=jnp.float32)
    g_s = g_q * t_rows
    g_t = g_q * s_wide
    return g_s, g_d, g_negrows, g_t


def bucket_grads(left, right, theta, src, dst, rel, neg, count):
    n_live = (count + SPAN - 1) // SPAN

    def step(c, carry):
        g_left, g_right, g_theta = carry
        mask = ((c * SPAN + jnp.arange(SPAN)) < count).astype(jnp.float32)
        g_s, g_d, g_negrows, g_t = span_grads(left, right, theta, src[c], dst[c], rel[c], neg[c], mask)
        g_left = g_left.at[src[c]].add(g_s)
        g_right = g_right.at[dst[c]].add(g_d).at[neg[c]].add(g_negrows)
        g_theta = g_theta.at[rel[c]].add(g_t)
        return g_left, g_right, g_theta

    init = (jnp.zeros((SLAB, W), jnp.float32), jnp.zeros((SLAB, W), jnp.float32), jnp.zeros((RELS, W), jnp.float32))
    return lax.fori_loop(0, n_live, step, init)


def reference(left_slab, right_slab, relation, src_ids, dst_ids, rel_ids, neg_ids, edge_counts):
    lefts = left_slab.reshape(GROUPS, SLAB, W)
    rights = right_slab.reshape(GROUPS, SLAB, W)
    theta = relation
    blocks = CAP // SPAN
    for rnd in range(ROUNDS):
        if rnd > 0:
            rights = jnp.roll(rights, 1, axis=0)
        src = src_ids[rnd].reshape(GROUPS, blocks, SPAN)
        dst = dst_ids[rnd].reshape(GROUPS, blocks, SPAN)
        rel = rel_ids[rnd].reshape(GROUPS, blocks, SPAN)
        neg = neg_ids[rnd]
        counts = edge_counts[rnd]

        def one_bucket(item):
            return bucket_grads(item[0], item[1], theta, item[2], item[3], item[4], item[5], item[6])

        g_left, g_right, g_theta = lax.map(one_bucket, (lefts, rights, src, dst, rel, neg, counts))
        lefts = (lefts.astype(jnp.float32) - learn_rate * g_left).astype(jnp.bfloat16)
        rights = (rights.astype(jnp.float32) - learn_rate * g_right).astype(jnp.bfloat16)
        theta = theta - relation_rate * jnp.sum(g_theta, axis=0)
    return lefts.reshape(GROUPS * SLAB, W), rights.reshape(GROUPS * SLAB, W), theta
```

```python
import functools

import jax
import jax.numpy as jnp
from jax import lax
from jax.experimental import pallas as pl
from jax.experimental.pallas import tpu as pltpu
from jax.sharding import PartitionSpec as P

MESH = pl.DeviceIdType.MESH
F32, BF16 = jnp.float32, jnp.bfloat16
learn_rate = 0.05
relation_rate = 0.05


def nn(a, b):
    return lax.dot_general(a, b, (((1,), (0,)), ((), ())), preferred_element_type=F32)


def nt(a, b):
    return lax.dot_general(a, b, (((1,), (1,)), ((), ())), preferred_element_type=F32)


def hot(ids, rows):
    return lax.broadcasted_iota(jnp.int32, (rows, ids.shape[1]), 0) == ids


def as_bf16(mask):
    return jnp.where(mask, 1.0, 0.0).astype(BF16)


def sigmoid(x):
    return 0.5 * jnp.tanh(0.5 * x) + 0.5


def kernel(
    cfg,
    count_ref, left_ref, right_ref, theta_ref, src_ref, dst_ref, rel_ref, neg_ref,
    left_out, right_out, theta_out,
    lf, rf, gl, gr, gt, counts, turned, left_t, right_t,
    gls, grs, glr, grr, moved, gts, pair_in, pair_sum, rs_in, ag,
    sem_l, sem_r, sem_gl, sem_gr, sem_pair, sem_rs, sem_ag, sem_fw,
):
    rounds, nb, ne, blocks, span, per, owners = cfg
    rows, width = left_ref.shape
    slab = rows * ne
    rels = theta_ref.shape[0]
    chips = nb // 2 * ne
    b, e = lax.axis_index("bucket"), lax.axis_index("edge")
    core = lax.rem(b, 2)
    chip = (b // 2) * ne + e
    mate = {"bucket": b + 1 - 2 * core, "edge": e}
    ahead, behind = lax.rem(b + 1, nb), lax.rem(b + nb - 1, nb)

    def chip_at(d):
        c = lax.rem(chip + d, chips)
        return c, {"bucket": 2 * (c // ne) + core, "edge": lax.rem(c, ne)}

    def edge_at(d):
        return lax.rem(e + d, ne)

    started = []

    def send(src, dst, sems, to):
        copy = pltpu.make_async_remote_copy(
            src_ref=src, dst_ref=dst, send_sem=sems.at[0], recv_sem=sems.at[1],
            device_id=to, device_id_type=MESH,
        )
        copy.start()
        started.append(copy)
        return copy

    barrier = pltpu.get_barrier_semaphore()
    for d in range(1, chips):
        pl.semaphore_signal(barrier, inc=1, device_id=chip_at(d)[1], device_id_type=MESH)
    for d in range(ne):
        for other in (ahead, behind):
            pl.semaphore_signal(
                barrier, inc=1, device_id={"bucket": other, "edge": edge_at(d)}, device_id_type=MESH
            )
    eye = as_bf16(
        lax.broadcasted_iota(jnp.int32, (width, width), 0) == lax.broadcasted_iota(jnp.int32, (width, width), 1)
    )
    lf[0, e] = left_ref[...]
    rf[0, e] = right_ref[...]
    pl.semaphore_wait(barrier, chips - 1 + 2 * ne)

    arrive = []
    for d in range(1, ne):
        to = {"bucket": b, "edge": edge_at(d)}
        arrive.append(send(left_ref, lf.at[0, e], sem_l.at[0, d], to))
        arrive.append(send(right_ref, rf.at[0, e], sem_r.at[0, d], to))

    def turn(theta):
        high = theta.astype(BF16)
        low = (theta - high.astype(F32)).astype(BF16)
        turned[pl.ds(0, width), :] = nt(eye, high).astype(BF16)
        turned[pl.ds(width, width), :] = nt(eye, low).astype(BF16)

    def count_round(r):
        ones = jnp.ones((neg_ref.shape[3], 128), BF16)

        def one(i, carry):
            ids = neg_ref[r, 0, pl.ds(i, 1), :]
            counts[r, i] = nn(as_bf16(hot(ids, slab)), ones)
            return carry

        lax.fori_loop(0, blocks, one, 0)

    turn(theta_ref[...])
    for r in range(rounds):
        count_round(r)

    edges = span * per

    for r in range(rounds):
        for copy in arrive:
            copy.wait_recv()
        arrive = []
        gl[...] = jnp.zeros_like(gl)
        gr[...] = jnp.zeros_like(gr)
        gt[...] = jnp.zeros_like(gt)
        left_t[...] = nt(eye, lf[r].reshape(slab, width)).astype(BF16)
        right_t[...] = nt(eye, rf[r].reshape(slab, width)).astype(BF16)
        live_to = count_ref[r, 0]

        def chunk(i, carry):
            at = pl.ds(pl.multiple_of(i * edges, edges), edges)
            src, dst, rel = src_ref[r, :, at], dst_ref[r, :, at], rel_ref[r, :, at]
            slot = (e * blocks + i * per) * span + lax.broadcasted_iota(jnp.int32, (1, edges), 1)
            live = jnp.where(slot < live_to, 1.0, 0.0)
            at_src = as_bf16(hot(src, slab))
            at_dst = hot(dst, slab)
            at_rel = as_bf16(hot(rel, rels))
            both = nn(turned[...], at_rel)
            t = both[:width] + both[width:]
            s = nn(left_t[...], at_src)
            q = (s * t).astype(BF16)
            scores = nn(rf[r].reshape(slab, width), q)
            pos = jnp.sum(jnp.where(at_dst, scores, 0.0), axis=0, keepdims=True)
            g_pos = -sigmoid(-pos) * live
            g_neg = (sigmoid(scores) * live).astype(BF16).astype(F32)
            many = jnp.concatenate(
                [counts[r, i * per + j] for j in range(per) for _ in range(span // 128)], axis=1
            )
            weight = (many * g_neg + jnp.where(at_dst, g_pos, 0.0)).astype(BF16)
            g_q = nn(right_t[...], weight)
            gr[...] += nt(weight, q).reshape(gr.shape)
            gl[...] += nt(at_src, (g_q * t).astype(BF16)).reshape(gl.shape)
            gt[...] += nt(at_rel, (g_q * s).astype(BF16)).reshape(gt.shape)
            return carry

        lax.fori_loop(0, blocks // per, chunk, 0)

        gts[r] = gt[...].astype(BF16).reshape(gts.shape[1:])
        pair = send(gts.at[r, 1 - core], pair_in.at[r], sem_pair.at[r], mate)
        gls[r] = gl[...].astype(BF16)
        grs[r] = gr[...].astype(BF16)
        slabs = []
        for d in range(1, ne):
            to = {"bucket": b, "edge": edge_at(d)}
            slabs.append(send(gls.at[r, edge_at(d)], glr.at[r, d], sem_gl.at[r, d], to))
            slabs.append(send(grs.at[r, edge_at(d)], grr.at[r, d], sem_gr.at[r, d], to))

        pair.wait_recv()
        pair_sum[r] = (gt[core].reshape(pair_sum.shape[1:]) + pair_in[r].astype(F32)).astype(BF16)
        parts = []

        def scatter(d):
            c, to = chip_at(d)
            return send(pair_sum.at[r, c], rs_in.at[r, d], sem_rs.at[r, d], to)

        if owners == chips:
            for d in range(1, chips):
                parts.append(scatter(d))
        else:
            for d in range(1, chips):
                @pl.when(chip_at(d)[0] < owners)
                def _():
                    scatter(d)
                    started.pop().wait_send()

        for copy in slabs:
            copy.wait_recv()
        new_l = lf[r, e].astype(F32)
        new_r = rf[r, e].astype(F32)
        g_l, g_r = gl[e], gr[e]
        for d in range(1, ne):
            g_l = g_l + glr[r, d].astype(F32)
            g_r = g_r + grr[r, d].astype(F32)
        new_l = (new_l - learn_rate * g_l).astype(BF16)
        new_r = (new_r - learn_rate * g_r).astype(BF16)
        if r == rounds - 1:
            left_out[...] = new_l
            right_out[...] = new_r
        else:
            lf[r + 1, e] = new_l
            moved[r] = new_r
            for d in range(ne):
                if d > 0:
                    to = {"bucket": b, "edge": edge_at(d)}
                    arrive.append(send(lf.at[r + 1, e], lf.at[r + 1, e], sem_l.at[r + 1, d], to))
                to = {"bucket": ahead, "edge": edge_at(d)}
                arrive.append(send(moved.at[r], rf.at[r + 1, e], sem_r.at[r + 1, d], to))

        def collect(d):
            return pltpu.make_async_remote_copy(
                src_ref=pair_sum.at[r, 0], dst_ref=rs_in.at[r, d], send_sem=sem_rs.at[r, d, 0],
                recv_sem=sem_rs.at[r, d, 1], device_id=mate, device_id_type=MESH,
            )

        def gathered(d):
            return pltpu.make_async_remote_copy(
                src_ref=pair_sum.at[r, 0], dst_ref=ag.at[r, core, 0], send_sem=sem_ag.at[r, d, 0],
                recv_sem=sem_ag.at[r, d, 1], device_id=mate, device_id_type=MESH,
            )

        def total():
            g = pair_sum[r, chip].astype(F32)
            for d in range(1, chips):
                g = g + rs_in[r, d].astype(F32)
            ag[r, core, chip] = g.astype(BF16)

        if owners == chips:
            for copy in parts:
                copy.wait_recv()
            total()
            parts = [
                send(ag.at[r, core, chip], ag.at[r, core, chip], sem_ag.at[r, d], chip_at(d)[1])
                for d in range(1, chips)
            ]
            for copy in parts:
                copy.wait_recv()
        else:
            @pl.when(chip < owners)
            def _():
                for d in range(1, chips):
                    collect(d).wait_recv()
                total()
                for d in range(1, chips):
                    send(ag.at[r, core, chip], ag.at[r, core, chip], sem_ag.at[r, d], chip_at(d)[1])
                    started.pop().wait_send()
            for d in range(1, chips):
                @pl.when(lax.rem(chip + chips - d, chips) < owners)
                def _():
                    gathered(d).wait_recv()

        send(ag.at[r, core], ag.at[r, core], sem_fw.at[r], mate).wait_recv()
        before = theta_ref[...] if r == 0 else theta_out[...]
        after = before - relation_rate * ag[r].astype(F32).reshape(rels, width)
        theta_out[...] = after
        if r < rounds - 1:
            turn(after)

    for copy in started:
        copy.wait_send()


def solution(mesh):
    nb, ne = mesh.shape["bucket"], mesh.shape["edge"]
    chips = nb // 2 * ne

    def body(left_slab, right_slab, relation, src_ids, dst_ids, rel_ids, neg_ids, edge_counts):
        rounds, _, blocks, _ = neg_ids.shape
        span = src_ids.shape[2] // blocks
        rows, width = left_slab.shape
        slab, rels = rows * ne, relation.shape[0]
        half = rels // 2
        per = 2 if slab <= 512 else 1
        owners = min(chips, half // 16)
        share = half // owners
        vmem = pl.BlockSpec(memory_space=pltpu.VMEM)
        dma = pltpu.SemaphoreType.DMA
        cfg = (rounds, nb, ne, blocks, span, per, owners)
        return pl.pallas_call(
            functools.partial(kernel, cfg),
            out_shape=(
                jax.ShapeDtypeStruct((rows, width), BF16),
                jax.ShapeDtypeStruct((rows, width), BF16),
                jax.ShapeDtypeStruct((rels, width), F32),
            ),
            in_specs=[pl.BlockSpec(memory_space=pltpu.SMEM)] + [vmem] * 7,
            out_specs=(vmem, vmem, vmem),
            scratch_shapes=[
                pltpu.VMEM((rounds, ne, rows, width), BF16),
                pltpu.VMEM((rounds, ne, rows, width), BF16),
                pltpu.VMEM((ne, rows, width), F32),
                pltpu.VMEM((ne, rows, width), F32),
                pltpu.VMEM((2, half, width), F32),
                pltpu.VMEM((rounds, blocks, slab, 128), F32),
                pltpu.VMEM((2 * width, rels), BF16),
                pltpu.VMEM((width, slab), BF16),
                pltpu.VMEM((width, slab), BF16),
                pltpu.VMEM((rounds, ne, rows, width), BF16),
                pltpu.VMEM((rounds, ne, rows, width), BF16),
                pltpu.VMEM((rounds, ne, rows, width), BF16),
                pltpu.VMEM((rounds, ne, rows, width), BF16),
                pltpu.VMEM((rounds, rows, width), BF16),
                pltpu.VMEM((rounds, 2, owners, share, width), BF16),
                pltpu.VMEM((rounds, owners, share, width), BF16),
                pltpu.VMEM((rounds, owners, share, width), BF16),
                pltpu.VMEM((rounds, chips, share, width), BF16),
                pltpu.VMEM((rounds, 2, owners, share, width), BF16),
                dma((rounds, ne, 2)),
                dma((rounds, ne, 2)),
                dma((rounds, ne, 2)),
                dma((rounds, ne, 2)),
                dma((rounds, 2)),
                dma((rounds, chips, 2)),
                dma((rounds, chips, 2)),
                dma((rounds, 2)),
            ],
            compiler_params=pltpu.CompilerParams(
                collective_id=0, has_side_effects=True, vmem_limit_bytes=60 * 1024 * 1024
            ),
        )(edge_counts, left_slab, right_slab, relation, src_ids, dst_ids, rel_ids, neg_ids)

    placed = (
        P(("bucket", "edge"), None),
        P(("bucket", "edge"), None),
        P(),
        P(None, "bucket", "edge"),
        P(None, "bucket", "edge"),
        P(None, "bucket", "edge"),
        P(None, "bucket", "edge", None),
        P(None, "bucket"),
    )
    return jax.shard_map(
        body,
        mesh=mesh,
        in_specs=placed,
        out_specs=(P(("bucket", "edge"), None), P(("bucket", "edge"), None), P()),
        check_vma=False,
    )
```

```python
import functools

import jax
import jax.numpy as jnp
from jax import lax
from jax.experimental import pallas as pl
from jax.experimental.pallas import tpu as pltpu
from jax.sharding import PartitionSpec as P

MESH = pl.DeviceIdType.MESH
F32, BF16 = jnp.float32, jnp.bfloat16
learn_rate = 0.05
relation_rate = 0.05


def nn(a, b):
    return lax.dot_general(a, b, (((1,), (0,)), ((), ())), preferred_element_type=F32)


def nt(a, b):
    return lax.dot_general(a, b, (((1,), (1,)), ((), ())), preferred_element_type=F32)


def hot(ids, rows):
    return lax.broadcasted_iota(jnp.int32, (rows, ids.shape[1]), 0) == ids


def as_bf16(mask):
    return jnp.where(mask, 1.0, 0.0).astype(BF16)


def sigmoid(x):
    return 0.5 * jnp.tanh(0.5 * x) + 0.5


def kernel(
    cfg,
    count_ref, left_ref, right_ref, theta_ref, src_ref, dst_ref, rel_ref, neg_ref,
    left_out, right_out, theta_out, step_out,
    lf, rf, gl, gr, gt, counts, turned, left_t, right_t,
    gls, grs, glr, grr, moved, gts, pair_in, pair_sum, rs_in, ag,
    sem_l, sem_r, sem_gl, sem_gr, sem_pair, sem_rs, sem_ag, sem_fw,
):
    rounds, nb, ne, blocks, span, per, owners, pieces = cfg
    rows, width = left_ref.shape
    slab = rows * ne
    rels = theta_ref.shape[0]
    half = rels // 2
    chips = nb // 2 * ne
    b, e = lax.axis_index("bucket"), lax.axis_index("edge")
    core = lax.rem(b, 2)
    chip = (b // 2) * ne + e
    mate = {"bucket": b + 1 - 2 * core, "edge": e}
    ahead, behind = lax.rem(b + 1, nb), lax.rem(b + nb - 1, nb)

    def chip_at(d):
        c = lax.rem(chip + d, chips)
        return c, {"bucket": 2 * (c // ne) + core, "edge": lax.rem(c, ne)}

    def edge_at(d):
        return lax.rem(e + d, ne)

    started = []

    def send(src, dst, sems, to):
        copy = pltpu.make_async_remote_copy(
            src_ref=src, dst_ref=dst, send_sem=sems.at[0], recv_sem=sems.at[1],
            device_id=to, device_id_type=MESH,
        )
        copy.start()
        started.append(copy)
        return copy

    barrier = pltpu.get_barrier_semaphore()
    for d in range(1, chips):
        pl.semaphore_signal(barrier, inc=1, device_id=chip_at(d)[1], device_id_type=MESH)
    for d in range(ne):
        for other in (ahead, behind):
            pl.semaphore_signal(
                barrier, inc=1, device_id={"bucket": other, "edge": edge_at(d)}, device_id_type=MESH
            )
    eye = as_bf16(
        lax.broadcasted_iota(jnp.int32, (width, width), 0) == lax.broadcasted_iota(jnp.int32, (width, width), 1)
    )
    lf[0, e] = left_ref[...]
    rf[0, e] = right_ref[...]
    pl.semaphore_wait(barrier, chips - 1 + 2 * ne)

    arrive = []
    for d in range(1, ne):
        to = {"bucket": b, "edge": edge_at(d)}
        arrive.append(send(left_ref, lf.at[0, e], sem_l.at[0, d], to))
        arrive.append(send(right_ref, rf.at[0, e], sem_r.at[0, d], to))

    def turn(theta):
        high = theta.astype(BF16)
        low = (theta - high.astype(F32)).astype(BF16)
        turned[pl.ds(0, width), :] = nt(eye, high).astype(BF16)
        turned[pl.ds(width, width), :] = nt(eye, low).astype(BF16)

    def count_round(r):
        ones = jnp.ones((neg_ref.shape[3], 128), BF16)

        def one(i, carry):
            ids = neg_ref[r, 0, pl.ds(i, 1), :]
            counts[r, i] = nn(as_bf16(hot(ids, slab)), ones)
            return carry

        lax.fori_loop(0, blocks, one, 0)

    turn(theta_ref[...])
    count_round(0)

    edges = span * per

    for r in range(rounds):
        for copy in arrive:
            copy.wait_recv()
        arrive = []
        gl[...] = jnp.zeros_like(gl)
        gr[...] = jnp.zeros_like(gr)
        gt[...] = jnp.zeros_like(gt)
        left_t[...] = nt(eye, lf[r].reshape(slab, width)).astype(BF16)
        right_t[...] = nt(eye, rf[r].reshape(slab, width)).astype(BF16)
        live_to = count_ref[0, r]

        def chunk(i, carry):
            at = pl.ds(pl.multiple_of(i * edges, edges), edges)
            src, dst, rel = src_ref[r, :, at], dst_ref[r, :, at], rel_ref[r, :, at]
            slot = (e * blocks + i * per) * span + lax.broadcasted_iota(jnp.int32, (1, edges), 1)
            live = jnp.where(slot < live_to, 1.0, 0.0)
            at_src = as_bf16(hot(src, slab))
            at_dst = hot(dst, slab)
            at_rel = as_bf16(hot(rel, rels))
            both = nn(turned[...], at_rel)
            t = both[:width] + both[width:]
            s = nn(left_t[...], at_src)
            q = (s * t).astype(BF16)
            scores = nn(rf[r].reshape(slab, width), q)
            pos = jnp.sum(jnp.where(at_dst, scores, 0.0), axis=0, keepdims=True)
            g_pos = -sigmoid(-pos) * live
            g_neg = (sigmoid(scores) * live).astype(BF16).astype(F32)
            many = jnp.concatenate(
                [counts[r, i * per + j] for j in range(per) for _ in range(span // 128)], axis=1
            )
            weight = (many * g_neg + jnp.where(at_dst, g_pos, 0.0)).astype(BF16)
            g_q = nn(right_t[...], weight)
            g_s = g_q * t
            gs = g_s.astype(BF16)
            gs_low = (g_s - gs.astype(F32)).astype(BF16)
            gr[...] += nt(weight, q).reshape(gr.shape)
            gl[...] += (nt(at_src, gs) + nt(at_src, gs_low)).reshape(gl.shape)
            gt[...] += nt(at_rel, (g_q * s).astype(BF16)).reshape(gt.shape)
            return carry

        lax.fori_loop(0, blocks // per, chunk, 0)

        for h in range(2):
            gts[r, h] = gt[h].astype(BF16).reshape(gts.shape[2:])
        pairs = [
            send(gts.at[r, 1 - core, p], pair_in.at[r, p], sem_pair.at[r, p], mate) for p in range(pieces)
        ]
        gls[r] = gl[...].astype(gls.dtype)
        grs[r] = gr[...].astype(grs.dtype)
        slabs = []
        for d in range(1, ne):
            to = {"bucket": b, "edge": edge_at(d)}
            slabs.append(send(gls.at[r, edge_at(d)], glr.at[r, d], sem_gl.at[r, d], to))
            slabs.append(send(grs.at[r, edge_at(d)], grr.at[r, d], sem_gr.at[r, d], to))

        def scatter(p, d):
            c, to = chip_at(d)
            return send(pair_sum.at[r, p, c], rs_in.at[r, p, d], sem_rs.at[r, p, d], to)

        def spread(p, d):
            block = ag.at[r, core, p, chip]
            return send(block, block, sem_ag.at[r, p, d], chip_at(d)[1])

        def total(p):
            g = pair_sum[r, p, chip].astype(F32)
            for d in range(1, chips):
                g = g + rs_in[r, p, d].astype(F32)
            ag[r, core, p, chip] = g.astype(BF16)

        def awaited(src, dst, sems):
            return pltpu.make_async_remote_copy(
                src_ref=src, dst_ref=dst, send_sem=sems.at[0], recv_sem=sems.at[1],
                device_id=mate, device_id_type=MESH,
            )

        scattered = []
        part = half // pieces
        for p in range(pieces):
            pairs[p].wait_recv()
            own = gt[core, pl.ds(p * part, part), :].reshape(pair_sum.shape[2:])
            pair_sum[r, p] = (own + pair_in[r, p].astype(F32)).astype(BF16)
            for d in range(1, chips):
                if owners == chips:
                    scattered.append(scatter(p, d))
                else:
                    @pl.when(chip_at(d)[0] < owners)
                    def _():
                        scatter(p, d)
                        started.pop().wait_send()

        if r < rounds - 1:
            count_round(r + 1)

        spreads = []
        for p in range(pieces):
            if owners == chips:
                for copy in scattered[p * (chips - 1):(p + 1) * (chips - 1)]:
                    copy.wait_recv()
                total(p)
                spreads.append([spread(p, d) for d in range(1, chips)])
            else:
                @pl.when(chip < owners)
                def _():
                    for d in range(1, chips):
                        awaited(pair_sum.at[r, p, 0], rs_in.at[r, p, d], sem_rs.at[r, p, d]).wait_recv()
                    total(p)
                    for d in range(1, chips):
                        spread(p, d)
                        started.pop().wait_send()

        for copy in slabs:
            copy.wait_recv()
        g_l, g_r = gl[e], gr[e]
        for d in range(1, ne):
            g_l = g_l + glr[r, d].astype(F32)
            g_r = g_r + grr[r, d].astype(F32)
        new_l = (lf[r, e].astype(F32) - learn_rate * g_l).astype(BF16)
        new_r = (rf[r, e].astype(F32) - learn_rate * g_r).astype(BF16)
        if r == rounds - 1:
            left_out[...] = new_l
            right_out[...] = new_r
        else:
            lf[r + 1, e] = new_l
            moved[r] = new_r
            for d in range(ne):
                if d > 0:
                    to = {"bucket": b, "edge": edge_at(d)}
                    arrive.append(send(lf.at[r + 1, e], lf.at[r + 1, e], sem_l.at[r + 1, d], to))
                to = {"bucket": ahead, "edge": edge_at(d)}
                arrive.append(send(moved.at[r], rf.at[r + 1, e], sem_r.at[r + 1, d], to))

        forwards = []
        for p in range(pieces):
            if owners == chips:
                for copy in spreads[p]:
                    copy.wait_recv()
            else:
                for d in range(1, chips):
                    @pl.when(lax.rem(chip + chips - d, chips) < owners)
                    def _():
                        awaited(pair_sum.at[r, p, 0], ag.at[r, core, p, 0], sem_ag.at[r, p, d]).wait_recv()
            forwards.append(send(ag.at[r, core, p], ag.at[r, core, p], sem_fw.at[r, p], mate))
        for copy in forwards:
            copy.wait_recv()
        if r == rounds - 1:
            step_out[...] = ag[r].reshape(rels, width)
        else:
            before = theta_ref[...] if r == 0 else theta_out[...]
            after = before - relation_rate * ag[r].astype(F32).reshape(rels, width)
            theta_out[...] = after
            turn(after)

    for copy in started:
        copy.wait_send()


def finish(left_ref, right_ref, theta_ref, step_ref, left_out, right_out, theta_out):
    left_out[...] = left_ref[...]
    right_out[...] = right_ref[...]
    theta_out[...] = theta_ref[...] - relation_rate * step_ref[...].astype(F32)


def solution(mesh):
    nb, ne = mesh.shape["bucket"], mesh.shape["edge"]
    chips = nb // 2 * ne

    def body(left_slab, right_slab, relation, src_ids, dst_ids, rel_ids, neg_ids, edge_counts):
        rounds, _, blocks, _ = neg_ids.shape
        span = src_ids.shape[2] // blocks
        rows, width = left_slab.shape
        slab, rels = rows * ne, relation.shape[0]
        half = rels // 2
        per = 4 if slab <= 512 else 1
        owners = min(chips, half // 16)
        pieces = max(1, min(1, half // (16 * owners)))
        share = half // owners // pieces
        vmem = pl.BlockSpec(memory_space=pltpu.VMEM)
        dma = pltpu.SemaphoreType.DMA
        cfg = (rounds, nb, ne, blocks, span, per, owners, pieces)
        left, right, theta, step = pl.pallas_call(
            functools.partial(kernel, cfg),
            out_shape=(
                jax.ShapeDtypeStruct((rows, width), BF16),
                jax.ShapeDtypeStruct((rows, width), BF16),
                jax.ShapeDtypeStruct((rels, width), F32),
                jax.ShapeDtypeStruct((rels, width), BF16),
            ),
            in_specs=[pl.BlockSpec(memory_space=pltpu.SMEM)] + [vmem] * 7,
            out_specs=(vmem, vmem, vmem, vmem),
            scratch_shapes=[
                pltpu.VMEM((rounds, ne, rows, width), BF16),
                pltpu.VMEM((rounds, ne, rows, width), BF16),
                pltpu.VMEM((ne, rows, width), F32),
                pltpu.VMEM((ne, rows, width), F32),
                pltpu.VMEM((2, half, width), F32),
                pltpu.VMEM((rounds, blocks, slab, 128), F32),
                pltpu.VMEM((2 * width, rels), BF16),
                pltpu.VMEM((width, slab), BF16),
                pltpu.VMEM((width, slab), BF16),
                pltpu.VMEM((rounds, ne, rows, width), BF16),
                pltpu.VMEM((rounds, ne, rows, width), BF16),
                pltpu.VMEM((rounds, ne, rows, width), BF16),
                pltpu.VMEM((rounds, ne, rows, width), BF16),
                pltpu.VMEM((rounds, rows, width), BF16),
                pltpu.VMEM((rounds, 2, pieces, owners, share, width), BF16),
                pltpu.VMEM((rounds, pieces, owners, share, width), BF16),
                pltpu.VMEM((rounds, pieces, owners, share, width), BF16),
                pltpu.VMEM((rounds, pieces, chips, share, width), BF16),
                pltpu.VMEM((rounds, 2, pieces, owners, share, width), BF16),
                dma((rounds, ne, 2)),
                dma((rounds, ne, 2)),
                dma((rounds, ne, 2)),
                dma((rounds, ne, 2)),
                dma((rounds, pieces, 2)),
                dma((rounds, pieces, chips, 2)),
                dma((rounds, pieces, chips, 2)),
                dma((rounds, pieces, 2)),
            ],
            compiler_params=pltpu.CompilerParams(
                collective_id=0, has_side_effects=True, vmem_limit_bytes=60 * 1024 * 1024
            ),
        )(edge_counts.T, left_slab, right_slab, relation, src_ids, dst_ids, rel_ids, neg_ids)
        return pl.pallas_call(
            finish,
            out_shape=(
                jax.ShapeDtypeStruct((rows, width), BF16),
                jax.ShapeDtypeStruct((rows, width), BF16),
                jax.ShapeDtypeStruct((rels, width), F32),
            ),
            in_specs=[vmem] * 4,
            out_specs=(vmem, vmem, vmem),
            compiler_params=pltpu.CompilerParams(vmem_limit_bytes=8 * 1024 * 1024),
        )(left, right, theta, step)

    placed = (
        P(("bucket", "edge"), None),
        P(("bucket", "edge"), None),
        P(),
        P(None, "bucket", "edge"),
        P(None, "bucket", "edge"),
        P(None, "bucket", "edge"),
        P(None, "bucket", "edge", None),
        P(None, "bucket"),
    )
    return jax.shard_map(
        body,
        mesh=mesh,
        in_specs=placed,
        out_specs=(P(("bucket", "edge"), None), P(("bucket", "edge"), None), P()),
        check_vma=False,
    )
```
